32 devices in a mesh: chan: 8 (over y, x, core), tm: 4 (over z).
Axes of the slice: x: 2, y: 2, z: 4, core: 2. Of those that a mesh axis runs over, the one named last changes fastest.
Arguments:
- records: float32 [2560, 4, 7936], P('chan', 'tm'), may hold values from -6 to 6
- offsets: int32 [4], P('tm'), may hold values from 0 to 256
Outputs:
- correlations: float32 [2, 640, 2, 20480], P(None, 'tm', None, 'chan')
The draws below stay inside these ranges and needn't reach their ends.
All inputs are finite; a program needn't handle non-finite values.
Results may differ from the reference program's by a relative error of at most 0.0001.
Values sent between devices are 32-bit elements; how exact they have to be, the bound alone decides.
A program may use at most 128 MiB of HBM per device.

```python
import jax
import jax.numpy as jnp
from jax import lax

CB = 320
SRC = 8
LEN = 7680
SLACK = 256
FB = 640
FLO = 64
SMOOTH = 64
ROUNDS = 2
SEG = 7936
CHANNELS = 2560
WINDOWS = 4
N_CHAN = 8


def draw_offsets(key, part):
    values = jax.random.randint(key, (WINDOWS,), 0, SLACK + 1)
    chosen = jax.random.randint(jax.random.fold_in(key, 11), (), 0, WINDOWS)
    values = values.at[chosen].set(SLACK)
    values = values.at[(chosen + 1) % WINDOWS].set(0)
    return values.astype(jnp.int32)


def level_of(stream_key, dims, shards, smallest, top_value):
    gain, own = 1.0, jax.random.fold_in(stream_key, 6)
    for position, blocks in shards:
        steps = jnp.exp(jax.random.uniform(jax.random.fold_in(own, position), (blocks,), jnp.float32, smallest / len(shards), top_value / len(shards)))
        gain = gain * jnp.repeat(steps, dims[position] // blocks).reshape([-1 if axis == position else 1 for axis in range(len(dims))])
    return gain


def centred(key, dims, scale, limit, pieces=(), kind=jnp.bfloat16):
    result = scale * jax.random.normal(key, dims, jnp.float32)
    if pieces:
        result = result * level_of(key, dims, pieces, -0.22, 0.18)
    return jnp.clip(result, -limit, limit).astype(kind)


def setup_inputs(seed: int = 0) -> dict:
    keys = jax.random.split(jax.random.key(seed), 3)
    records = centred(keys[0], (CHANNELS, WINDOWS, SEG), 1.0, 6.0, ((0, 8), (1, 4)), jnp.float32)
    offsets = draw_offsets(jax.random.fold_in(keys[2], 71), 0)
    return {"records": records, "offsets": offsets}


def whiten_block(block, offsets):

    def cut(rec, off):
        return lax.dynamic_slice_in_dim(rec, off, LEN, 1)
    windows = jax.vmap(cut, in_axes=(1, 0), out_axes=1)(block, offsets.astype(jnp.int32))
    spectrum = jnp.fft.rfft(windows, axis=-1)[..., FLO:FLO + FB]
    spec_re = jnp.real(spectrum)
    spec_im = jnp.imag(spectrum)
    amplitude = jnp.sqrt(spec_re * spec_re + spec_im * spec_im)
    bins = jnp.arange(FB)
    kernel = (jnp.abs(bins[:, None] - bins[None, :]) <= SMOOTH).astype(amplitude.dtype)
    counts = lax.optimization_barrier(jnp.sum(kernel, axis=0))
    smooth = jnp.einsum('cwk,kl->cwl', amplitude, kernel, precision=lax.Precision.HIGHEST) / counts
    scale = 1.0 / (smooth + 1e-06)
    return jnp.stack([spec_re * scale, spec_im * scale], axis=2)

def reference(records, offsets):
    blocks = records.reshape(N_CHAN, CB, WINDOWS, SEG)
    white = lax.map(lambda blk: whiten_block(blk, offsets), blocks)
    hp = lax.Precision.HIGHEST
    results = []
    for rnd in range(1, ROUNDS + 1):
        partner = jnp.roll(white, -rnd, axis=0)[:, :SRC]
        ar, ai = (white[:, :, :, 0], white[:, :, :, 1])
        br, bi = (partner[:, :, :, 0], partner[:, :, :, 1])
        real_part = jnp.einsum('biwf,bjwf->bfij', ar, br, precision=hp) + jnp.einsum('biwf,bjwf->bfij', ai, bi, precision=hp)
        imag_part = jnp.einsum('biwf,bjwf->bfij', ai, br, precision=hp) - jnp.einsum('biwf,bjwf->bfij', ar, bi, precision=hp)
        both = jnp.stack([real_part, imag_part], axis=2) / WINDOWS
        both = jnp.transpose(both, (1, 2, 0, 3, 4)).reshape(FB, 2, N_CHAN * CB * SRC)
        results.append(both)
    return jnp.stack(results, axis=0)
```

```python
import functools
import math

import jax
import jax.numpy as jnp
import numpy as np
from jax import lax
from jax.experimental import pallas as pl
from jax.experimental.pallas import tpu as pltpu
from jax.sharding import PartitionSpec as P

SRC = 8
LEN = 7680
FB = 640
FLO = 64
SMOOTH = 64
ROUNDS = 2
M = 15
L = LEN // M
Q0 = FLO // M
NQ = 48
BASE = 16
START = BASE + M * Q0 - FLO
ROWS = START + M // 2 + M * (NQ - 1) + 5
LANES = 128
PARTS = LEN // LANES


def split(x):
    hi = x.astype(jnp.bfloat16)
    return hi, (x - hi.astype(jnp.float32)).astype(jnp.bfloat16)


def tables():
    a = np.arange(L)
    q = Q0 + np.arange(NQ)
    angle = 2.0 * math.pi * ((q[:, None] * a[None, :]) % L) / L
    full = np.concatenate([np.cos(angle), np.sin(angle)]).astype(np.float32)
    hi = full.astype(jnp.bfloat16)
    lo = (full - hi.astype(np.float32)).astype(jnp.bfloat16)
    both = np.concatenate([hi, lo])
    r = np.arange(1, M // 2 + 1)
    turn = 2.0 * math.pi * (r[:, None] * a[None, :]) / LEN
    twiddle = np.stack([np.cos(turn), np.sin(turn)], 1).reshape(2 * len(r), L)
    twiddle = np.repeat(twiddle[:, None, :], 8, 1).astype(np.float32)
    k = np.arange(FB)
    band = (np.abs(k[:, None] - k[None, :]) <= SMOOTH).astype(jnp.bfloat16)
    return both, twiddle, band


C3 = math.sqrt(3.0) / 2.0
C51, C52 = math.cos(2 * math.pi / 5), math.cos(4 * math.pi / 5)
S51, S52 = math.sin(2 * math.pi / 5), math.sin(4 * math.pi / 5)


def dft3(x0, x1, x2):
    t = x1 + x2
    return x0 + t, x0 - 0.5 * t, C3 * (x2 - x1)


def dft5(x):
    t1, t2 = x[1] + x[4], x[2] + x[3]
    d1, d2 = x[1] - x[4], x[2] - x[3]
    re0 = x[0] + t1 + t2
    re1 = x[0] + C51 * t1 + C52 * t2
    re2 = x[0] + C52 * t1 + C51 * t2
    im1 = -(S51 * d1 + S52 * d2)
    im2 = S51 * d2 - S52 * d1
    return re0, re1, im1, re2, im2


def dft15(x):
    columns = [dft3(*[x[(5 * n1 + 3 * n2) % 15] for n1 in range(3)]) for n2 in range(5)]
    z = dft5([c[0] for c in columns])
    u = dft5([c[1] for c in columns])
    v = dft5([c[2] for c in columns])
    out = {}
    out[(0, 0)] = (z[0], None)
    out[(0, 1)] = (z[1], z[2])
    out[(0, 2)] = (z[3], z[4])
    out[(1, 0)] = (u[0], v[0])
    for j, (b, s) in ((1, (1, 2)), (2, (3, 4))):
        out[(1, j)] = (u[b] - v[s], u[s] + v[b])
        out[(1, 5 - j)] = (u[b] + v[s], v[b] - u[s])
    bins = [None] * 8
    for (k1, k2), (re, im) in out.items():
        k = (10 * k1 + 6 * k2) % 15
        if k <= 7:
            bins[k] = (re, im)
        else:
            bins[15 - k] = (re, -im)
    return bins


def spectra(rows, off_ref, x_ref, both_ref, twiddle_ref, band_ref, o_ref, hi_ref, lo_ref, re_ref, im_ref):
    step = pl.program_id(0)
    off = off_ref[0]
    lane = lax.broadcasted_iota(jnp.int32, (16, LANES), 1)

    def put(row, c0, a0, value):
        hi, lo = split(value)
        hi_ref[pl.ds(row * LANES + c0, 16), pl.ds(a0, LANES)] = hi
        lo_ref[pl.ds(row * LANES + c0, 16), pl.ds(a0, LANES)] = lo

    extra = rows - PARTS

    def block(i, carry):
        c0 = pl.multiple_of(i * 16, 16)

        def load(j):
            return x_ref[pl.ds(c0 * rows + j, 16, stride=rows), :]

        for t in range(L // LANES):
            x = []
            for b in range(M):
                j = b * (L // LANES) + t
                value = load(j)
                if j < extra:
                    value = jnp.where(lane + j * LANES < off, load(j + PARTS), value)
                x.append(value)
            bins = dft15(x)
            a0 = t * LANES
            put(0, c0, a0, bins[0][0])
            for r in range(1, 8):
                re, im = bins[r]
                cos = twiddle_ref[2 * r - 2, :, a0 : a0 + LANES]
                sin = twiddle_ref[2 * r - 1, :, a0 : a0 + LANES]
                cos = jnp.concatenate([cos, cos], 0)
                sin = jnp.concatenate([sin, sin], 0)
                put(2 * r - 1, c0, a0, re * cos + im * sin)
                put(2 * r, c0, a0, im * cos - re * sin)
        return carry

    lax.fori_loop(0, LANES // 16, block, 0)

    nt = (((1,), (1,)), ((), ()))

    def second(row, count):
        window = slice(row * LANES, (row + count) * LANES)
        p = lax.dot_general(both_ref[...], hi_ref[window, :], nt, preferred_element_type=jnp.float32)
        s = lax.dot_general(both_ref[: 2 * NQ, :], lo_ref[window, :], nt, preferred_element_type=jnp.float32)
        return p[: 2 * NQ] + p[2 * NQ :] + s

    z = second(0, 1)
    re_ref[pl.ds(START, NQ, stride=M), :] = z[:NQ]
    im_ref[pl.ds(START, NQ, stride=M), :] = -z[NQ:]
    for r in range(1, 8):
        z = second(2 * r - 1, 2)
        rc, rs = z[:NQ, :LANES], z[NQ:, :LANES]
        ic, is_ = z[:NQ, LANES:], z[NQ:, LANES:]
        re_ref[pl.ds(START + r, NQ, stride=M), :] = rc + is_
        im_ref[pl.ds(START + r, NQ, stride=M), :] = ic - rs
        re_ref[pl.ds(START - r, NQ, stride=M), :] = rc - is_
        im_ref[pl.ds(START - r, NQ, stride=M), :] = -ic - rs
    re = re_ref[BASE : BASE + FB, :]
    im = im_ref[BASE : BASE + FB, :]
    hi, lo = split(jnp.sqrt(re * re + im * im))
    total = jnp.dot(band_ref[...], jnp.concatenate([hi, lo], 1), preferred_element_type=jnp.float32)
    k = lax.broadcasted_iota(jnp.int32, (FB, LANES), 0)
    count = jnp.minimum(k + SMOOTH, FB - 1) - jnp.maximum(k - SMOOTH, 0) + 1
    smooth = (total[:, :LANES] + total[:, LANES:]) / count.astype(jnp.float32)
    scale = 1.0 / (smooth + 1e-06)
    re, im = re * scale, im * scale
    whole = pl.num_programs(0) - 1

    @pl.when(step < whole)
    def _():
        o_ref[:, :LANES] = re
        o_ref[:, LANES:] = im

    @pl.when(step == whole)
    def _():
        low = lax.broadcasted_iota(jnp.int32, (FB, LANES), 1) < LANES // 2
        o_ref[:, :LANES] = jnp.where(low, re, pltpu.roll(im, LANES // 2, 1))


def whiten(records, offsets):
    chans = records.shape[0]
    rows = records.shape[2] // LANES
    flat = records.reshape(chans * rows, LANES)
    both, twiddle, band = tables()
    steps = -(-chans // LANES)
    keep = lambda shape: pl.BlockSpec(shape, lambda i: (0,) * len(shape))
    return pl.pallas_call(
        functools.partial(spectra, rows),
        grid=(steps,),
        in_specs=[
            pl.BlockSpec(memory_space=pltpu.SMEM),
            pl.BlockSpec((LANES * rows, LANES), lambda i: (i, 0)),
            keep(both.shape),
            keep(twiddle.shape),
            keep(band.shape),
        ],
        out_specs=pl.BlockSpec((FB, 2 * LANES), lambda i: (0, i)),
        out_shape=jax.ShapeDtypeStruct((FB, 2 * chans), jnp.float32),
        scratch_shapes=[
            pltpu.VMEM((M * LANES, L), jnp.bfloat16),
            pltpu.VMEM((M * LANES, L), jnp.bfloat16),
            pltpu.VMEM((ROWS + 8, LANES), jnp.float32),
            pltpu.VMEM((ROWS + 8, LANES), jnp.float32),
        ],
        compiler_params=pltpu.CompilerParams(vmem_limit_bytes=48 << 20),
        name="whiten",
    )(offsets, flat, jnp.asarray(both), jnp.asarray(twiddle), jnp.asarray(band))


KB = 8


def pairing(wins, chans, scale, a_ref, b_ref, e_ref, o_ref, x_ref):
    tiles = chans * SRC // LANES
    per = LANES // SRC
    full = chans // LANES
    for t in range(-(-chans // LANES)):
        if t < full:
            re = a_ref[:, :, 2 * t * LANES : (2 * t + 1) * LANES]
            im = a_ref[:, :, (2 * t + 1) * LANES : (2 * t + 2) * LANES]
            width = LANES * SRC
        else:
            re = a_ref[:, :, 2 * t * LANES : (2 * t + 1) * LANES]
            im = pltpu.roll(re, LANES // 2, 2)
            width = LANES * SRC // 2
        both = jnp.concatenate([re, im], 0).reshape(2 * wins * KB, LANES)
        hi, lo = split(both)
        lhs = jnp.concatenate([hi, lo], 1)
        x_ref[:, t * LANES * SRC : t * LANES * SRC + width] = jnp.dot(
            lhs, e_ref[:, :width], preferred_element_type=jnp.float32
        )
    for tile in range(tiles):
        lanes = slice(tile * LANES, (tile + 1) * LANES)
        ar = [x_ref[w * KB : (w + 1) * KB, lanes] for w in range(wins)]
        ai = [x_ref[(wins + w) * KB : (wins + w + 1) * KB, lanes] for w in range(wins)]
        for rnd in range(ROUNDS):
            real = imag = None
            for w in range(wins):
                br, bi = b_ref[rnd, w, 0], b_ref[rnd, w, 1]
                p = ar[w] * br + ai[w] * bi
                q = ai[w] * br - ar[w] * bi
                real = p if real is None else real + p
                imag = q if imag is None else imag + q
            o_ref[rnd, pl.ds(2 * tile, KB, stride=2 * tiles), :] = real * scale
            o_ref[rnd, pl.ds(2 * tile + 1, KB, stride=2 * tiles), :] = imag * scale


def correlate(grouped, sources):
    wins, bins, wide = grouped.shape
    chans = wide // 2
    tiles = chans * SRC // LANES
    spread = (np.arange(LANES)[:, None] == np.arange(LANES * SRC)[None, :] // SRC).astype(jnp.bfloat16)
    spread = np.concatenate([spread, spread])
    out = pl.pallas_call(
        functools.partial(pairing, wins, chans, 1.0 / wins),
        grid=(bins // KB,),
        in_specs=[
            pl.BlockSpec((wins, KB, wide), lambda i: (0, i, 0)),
            pl.BlockSpec((ROUNDS, wins, 2, KB, LANES), lambda i: (0, 0, 0, i, 0)),
            pl.BlockSpec(spread.shape, lambda i: (0, 0)),
        ],
        out_specs=pl.BlockSpec((ROUNDS, KB * tiles * 2, LANES), lambda i: (0, i, 0)),
        out_shape=jax.ShapeDtypeStruct((ROUNDS, bins * tiles * 2, LANES), jnp.float32),
        scratch_shapes=[pltpu.VMEM((2 * wins * KB, chans * SRC), jnp.float32)],
        compiler_params=pltpu.CompilerParams(vmem_limit_bytes=48 << 20),
        name="pairing",
    )(grouped, sources, jnp.asarray(spread))
    out = out.reshape(ROUNDS, bins, tiles, 2, LANES).transpose(0, 1, 3, 2, 4)
    return out.reshape(ROUNDS, bins, 2, tiles * LANES)


def passed_along(block, axis, distance):
    devices = range(lax.axis_size(axis))
    route = [((i - distance) % len(devices), i) for i in devices]
    return lax.ppermute(block, axis, route)


def shards(records, offsets):
    wins = records.shape[1]
    assert wins == 1
    white = whiten(records, offsets)
    n = lax.axis_size("tm")
    grouped = lax.all_to_all(white.reshape(n, FB // n, white.shape[1]), "tm", split_axis=0, concat_axis=0)
    own = jnp.stack([grouped[:, :, :SRC], grouped[:, :, LANES : LANES + SRC]], 1)
    shape = own.shape
    flat = own.reshape(-1, LANES)
    got = [passed_along(flat, "chan", -rnd).reshape(shape) for rnd in range(1, ROUNDS + 1)]
    sources = jnp.tile(jnp.stack(got), (1, 1, 1, 1, LANES // SRC))
    return correlate(grouped, sources)


def solution(mesh):
    return jax.shard_map(
        shards,
        mesh=mesh,
        in_specs=(P("chan", "tm", None), P("tm")),
        out_specs=P(None, "tm", None, "chan"),
        check_vma=False,
    )
```

```python
import functools
import math

import jax
import jax.numpy as jnp
import numpy as np
from jax import lax
from jax.experimental import pallas as pl
from jax.experimental.pallas import tpu as pltpu
from jax.sharding import PartitionSpec as P

SRC = 8
LEN = 7680
FB = 640
FLO = 64
SMOOTH = 64
ROUNDS = 2
M = 15
L = LEN // M
Q0 = FLO // M
NQ = 48
BASE = 16
START = BASE + M * Q0 - FLO
ROWS = START + M // 2 + M * (NQ - 1) + 5
LANES = 128
PARTS = LEN // LANES


def split(x):
    hi = x.astype(jnp.bfloat16)
    return hi, (x - hi.astype(jnp.float32)).astype(jnp.bfloat16)


def tables():
    a = np.arange(L)
    q = Q0 + np.arange(NQ)
    angle = 2.0 * math.pi * ((q[:, None] * a[None, :]) % L) / L
    full = np.concatenate([np.cos(angle), np.sin(angle)]).astype(np.float32)
    hi = full.astype(jnp.bfloat16)
    lo = (full - hi.astype(np.float32)).astype(jnp.bfloat16)
    both = np.concatenate([hi, lo])
    r = np.arange(1, M // 2 + 1)
    turn = 2.0 * math.pi * (r[:, None] * a[None, :]) / LEN
    twiddle = np.stack([np.cos(turn), np.sin(turn)], 1).reshape(2 * len(r), L)
    twiddle = np.repeat(twiddle[:, None, :], 8, 1).astype(np.float32)
    k = np.arange(FB)
    band = (np.abs(k[:, None] - k[None, :]) <= SMOOTH).astype(jnp.bfloat16)
    return both, twiddle, band


C3 = math.sqrt(3.0) / 2.0
C51, C52 = math.cos(2 * math.pi / 5), math.cos(4 * math.pi / 5)
S51, S52 = math.sin(2 * math.pi / 5), math.sin(4 * math.pi / 5)


def dft3(x0, x1, x2):
    t = x1 + x2
    return x0 + t, x0 - 0.5 * t, C3 * (x2 - x1)


def dft5(x):
    t1, t2 = x[1] + x[4], x[2] + x[3]
    d1, d2 = x[1] - x[4], x[2] - x[3]
    re0 = x[0] + t1 + t2
    re1 = x[0] + C51 * t1 + C52 * t2
    re2 = x[0] + C52 * t1 + C51 * t2
    im1 = -(S51 * d1 + S52 * d2)
    im2 = S51 * d2 - S52 * d1
    return re0, re1, im1, re2, im2


def dft15(x):
    columns = [dft3(*[x[(5 * n1 + 3 * n2) % 15] for n1 in range(3)]) for n2 in range(5)]
    z = dft5([c[0] for c in columns])
    u = dft5([c[1] for c in columns])
    v = dft5([c[2] for c in columns])
    out = {}
    out[(0, 0)] = (z[0], None)
    out[(0, 1)] = (z[1], z[2])
    out[(0, 2)] = (z[3], z[4])
    out[(1, 0)] = (u[0], v[0])
    for j, (b, s) in ((1, (1, 2)), (2, (3, 4))):
        out[(1, j)] = (u[b] - v[s], u[s] + v[b])
        out[(1, 5 - j)] = (u[b] + v[s], v[b] - u[s])
    bins = [None] * 8
    for (k1, k2), (re, im) in out.items():
        k = (10 * k1 + 6 * k2) % 15
        if k <= 7:
            bins[k] = (re, im)
        else:
            bins[15 - k] = (re, -im)
    return bins


def spectra(rows, off_ref, x_ref, both_ref, twiddle_ref, band_ref, o_ref, hi_ref, lo_ref, re_ref, im_ref):
    step = pl.program_id(0)
    off = off_ref[0]
    lane = lax.broadcasted_iota(jnp.int32, (16, LANES), 1)

    def put(row, c0, a0, value):
        hi, lo = split(value)
        hi_ref[pl.ds(row * LANES + c0, 16), pl.ds(a0, LANES)] = hi
        lo_ref[pl.ds(row * LANES + c0, 16), pl.ds(a0, LANES)] = lo

    extra = rows - PARTS

    def block(i, carry):
        c0 = pl.multiple_of(i * 16, 16)

        def load(j):
            return x_ref[pl.ds(c0 * rows + j, 16, stride=rows), :]

        for t in range(L // LANES):
            x = []
            for b in range(M):
                j = b * (L // LANES) + t
                value = load(j)
                if j < extra:
                    value = jnp.where(lane + j * LANES < off, load(j + PARTS), value)
                x.append(value)
            bins = dft15(x)
            a0 = t * LANES
            put(0, c0, a0, bins[0][0])
            for r in range(1, 8):
                re, im = bins[r]
                cos = twiddle_ref[2 * r - 2, :, a0 : a0 + LANES]
                sin = twiddle_ref[2 * r - 1, :, a0 : a0 + LANES]
                cos = jnp.concatenate([cos, cos], 0)
                sin = jnp.concatenate([sin, sin], 0)
                put(2 * r - 1, c0, a0, re * cos + im * sin)
                put(2 * r, c0, a0, im * cos - re * sin)
        return carry

    lax.fori_loop(0, LANES // 16, block, 0)

    nt = (((1,), (1,)), ((), ()))

    def second(row, count):
        window = slice(row * LANES, (row + count) * LANES)
        p = lax.dot_general(both_ref[...], hi_ref[window, :], nt, preferred_element_type=jnp.float32)
        s = lax.dot_general(both_ref[: 2 * NQ, :], lo_ref[window, :], nt, preferred_element_type=jnp.float32)
        return p[: 2 * NQ] + p[2 * NQ :] + s

    z = second(0, 1)
    re_ref[pl.ds(START, NQ, stride=M), :] = z[:NQ]
    im_ref[pl.ds(START, NQ, stride=M), :] = -z[NQ:]
    for r in range(1, 8):
        z = second(2 * r - 1, 2)
        rc, rs = z[:NQ, :LANES], z[NQ:, :LANES]
        ic, is_ = z[:NQ, LANES:], z[NQ:, LANES:]
        re_ref[pl.ds(START + r, NQ, stride=M), :] = rc + is_
        im_ref[pl.ds(START + r, NQ, stride=M), :] = ic - rs
        re_ref[pl.ds(START - r, NQ, stride=M), :] = rc - is_
        im_ref[pl.ds(START - r, NQ, stride=M), :] = -ic - rs
    re = re_ref[BASE : BASE + FB, :]
    im = im_ref[BASE : BASE + FB, :]
    hi, lo = split(jnp.sqrt(re * re + im * im))
    total = jnp.dot(band_ref[...], jnp.concatenate([hi, lo], 1), preferred_element_type=jnp.float32)
    k = lax.broadcasted_iota(jnp.int32, (FB, LANES), 0)
    count = jnp.minimum(k + SMOOTH, FB - 1) - jnp.maximum(k - SMOOTH, 0) + 1
    smooth = (total[:, :LANES] + total[:, LANES:]) / count.astype(jnp.float32)
    scale = 1.0 / (smooth + 1e-06)
    re, im = re * scale, im * scale
    whole = pl.num_programs(0) - 1

    @pl.when(step < whole)
    def _():
        o_ref[:, :LANES] = re
        o_ref[:, LANES:] = im

    @pl.when(step == whole)
    def _():
        low = lax.broadcasted_iota(jnp.int32, (FB, LANES), 1) < LANES // 2
        o_ref[:, :LANES] = jnp.where(low, re, pltpu.roll(im, LANES // 2, 1))


def whiten(records, offsets):
    chans = records.shape[0]
    rows = records.shape[2] // LANES
    flat = records.reshape(chans * rows, LANES)
    both, twiddle, band = tables()
    steps = -(-chans // LANES)
    keep = lambda shape: pl.BlockSpec(shape, lambda i: (0,) * len(shape))
    return pl.pallas_call(
        functools.partial(spectra, rows),
        grid=(steps,),
        in_specs=[
            pl.BlockSpec(memory_space=pltpu.SMEM),
            pl.BlockSpec((LANES * rows, LANES), lambda i: (i, 0)),
            keep(both.shape),
            keep(twiddle.shape),
            keep(band.shape),
        ],
        out_specs=pl.BlockSpec((FB, 2 * LANES), lambda i: (0, i)),
        out_shape=jax.ShapeDtypeStruct((FB, 2 * chans), jnp.float32),
        scratch_shapes=[
            pltpu.VMEM((M * LANES, L), jnp.bfloat16),
            pltpu.VMEM((M * LANES, L), jnp.bfloat16),
            pltpu.VMEM((ROWS + 8, LANES), jnp.float32),
            pltpu.VMEM((ROWS + 8, LANES), jnp.float32),
        ],
        compiler_params=pltpu.CompilerParams(vmem_limit_bytes=48 << 20),
        name="whiten",
    )(offsets, flat, jnp.asarray(both), jnp.asarray(twiddle), jnp.asarray(band))


KB = 8


def pairing(wins, chans, scale, a_ref, b_ref, e_ref, o_ref, x_ref):
    tiles = chans * SRC // LANES
    per = LANES // SRC
    full = chans // LANES
    for t in range(-(-chans // LANES)):
        if t < full:
            re = a_ref[:, :, 2 * t * LANES : (2 * t + 1) * LANES]
            im = a_ref[:, :, (2 * t + 1) * LANES : (2 * t + 2) * LANES]
            width = LANES * SRC
        else:
            re = a_ref[:, :, 2 * t * LANES : (2 * t + 1) * LANES]
            im = pltpu.roll(re, LANES // 2, 2)
            width = LANES * SRC // 2
        both = jnp.concatenate([re, im], 0).reshape(2 * wins * KB, LANES)
        hi, lo = split(both)
        lhs = jnp.concatenate([hi, lo], 1)
        x_ref[:, t * LANES * SRC : t * LANES * SRC + width] = jnp.dot(
            lhs, e_ref[:, :width], preferred_element_type=jnp.float32
        )
    for tile in range(tiles):
        lanes = slice(tile * LANES, (tile + 1) * LANES)
        ar = [x_ref[w * KB : (w + 1) * KB, lanes] for w in range(wins)]
        ai = [x_ref[(wins + w) * KB : (wins + w + 1) * KB, lanes] for w in range(wins)]
        for rnd in range(ROUNDS):
            real = imag = None
            for w in range(wins):
                br, bi = b_ref[rnd, w, 0], b_ref[rnd, w, 1]
                p = ar[w] * br + ai[w] * bi
                q = ai[w] * br - ar[w] * bi
                real = p if real is None else real + p
                imag = q if imag is None else imag + q
            o_ref[rnd, :, 0, lanes] = real * scale
            o_ref[rnd, :, 1, lanes] = imag * scale


def correlate(grouped, sources):
    wins, bins, wide = grouped.shape
    chans = wide // 2
    tiles = chans * SRC // LANES
    spread = (np.arange(LANES)[:, None] == np.arange(LANES * SRC)[None, :] // SRC).astype(jnp.bfloat16)
    spread = np.concatenate([spread, spread])
    out = pl.pallas_call(
        functools.partial(pairing, wins, chans, 1.0 / wins),
        grid=(bins // KB,),
        in_specs=[
            pl.BlockSpec((wins, KB, wide), lambda i: (0, i, 0)),
            pl.BlockSpec((ROUNDS, wins, 2, KB, LANES), lambda i: (0, 0, 0, i, 0)),
            pl.BlockSpec(spread.shape, lambda i: (0, 0)),
        ],
        out_specs=pl.BlockSpec((ROUNDS, KB, 2, chans * SRC), lambda i: (0, i, 0, 0)),
        out_shape=jax.ShapeDtypeStruct((ROUNDS, bins, 2, chans * SRC), jnp.float32),
        scratch_shapes=[pltpu.VMEM((2 * wins * KB, chans * SRC), jnp.float32)],
        compiler_params=pltpu.CompilerParams(vmem_limit_bytes=48 << 20),
        name="pairing",
    )(grouped, sources, jnp.asarray(spread))
    return out


def passed_along(block, axis, distance):
    devices = range(lax.axis_size(axis))
    route = [((i - distance) % len(devices), i) for i in devices]
    return lax.ppermute(block, axis, route)


def shards(records, offsets):
    wins = records.shape[1]
    assert wins == 1
    white = whiten(records, offsets)
    n = lax.axis_size("tm")
    grouped = lax.all_to_all(white.reshape(n, FB // n, white.shape[1]), "tm", split_axis=0, concat_axis=0)
    own = jnp.stack([grouped[:, :, :SRC], grouped[:, :, LANES : LANES + SRC]], 1)
    shape = own.shape
    flat = own.reshape(-1, LANES)
    got = [passed_along(flat, "chan", -rnd).reshape(shape) for rnd in range(1, ROUNDS + 1)]
    sources = jnp.tile(jnp.stack(got), (1, 1, 1, 1, LANES // SRC))
    return correlate(grouped, sources)


def solution(mesh):
    return jax.shard_map(
        shards,
        mesh=mesh,
        in_specs=(P("chan", "tm", None), P("tm")),
        out_specs=P(None, "tm", None, "chan"),
        check_vma=False,
    )
```

```python
import functools
import math

import jax
import jax.numpy as jnp
import numpy as np
from jax import lax
from jax.experimental import pallas as pl
from jax.experimental.pallas import tpu as pltpu
from jax.sharding import PartitionSpec as P

SRC = 8
LEN = 7680
FB = 640
FLO = 64
SMOOTH = 64
ROUNDS = 2
M = 15
L = LEN // M
Q0 = FLO // M
NQ = 48
BASE = 16
START = BASE + M * Q0 - FLO
ROWS = START + M // 2 + M * (NQ - 1) + 5
LANES = 128
PARTS = LEN // LANES


def split(x):
    hi = x.astype(jnp.bfloat16)
    return hi, (x - hi.astype(jnp.float32)).astype(jnp.bfloat16)


def tables():
    a = np.arange(L)
    q = Q0 + np.arange(NQ)
    angle = 2.0 * math.pi * ((q[:, None] * a[None, :]) % L) / L
    full = np.concatenate([np.cos(angle), np.sin(angle)]).astype(np.float32)
    hi = full.astype(jnp.bfloat16)
    lo = (full - hi.astype(np.float32)).astype(jnp.bfloat16)
    both = np.concatenate([hi, lo])
    r = np.arange(1, M // 2 + 1)
    turn = 2.0 * math.pi * (r[:, None] * a[None, :]) / LEN
    twiddle = np.stack([np.cos(turn), np.sin(turn)], 1).reshape(2 * len(r), L)
    twiddle = np.repeat(twiddle[:, None, :], 8, 1).astype(np.float32)
    k = np.arange(FB)
    band = (np.abs(k[:, None] - k[None, :]) <= SMOOTH).astype(jnp.bfloat16)
    return both, twiddle, band


C3 = math.sqrt(3.0) / 2.0
C51, C52 = math.cos(2 * math.pi / 5), math.cos(4 * math.pi / 5)
S51, S52 = math.sin(2 * math.pi / 5), math.sin(4 * math.pi / 5)


def dft3(x0, x1, x2):
    t = x1 + x2
    return x0 + t, x0 - 0.5 * t, C3 * (x2 - x1)


def dft5(x):
    t1, t2 = x[1] + x[4], x[2] + x[3]
    d1, d2 = x[1] - x[4], x[2] - x[3]
    re0 = x[0] + t1 + t2
    re1 = x[0] + C51 * t1 + C52 * t2
    re2 = x[0] + C52 * t1 + C51 * t2
    im1 = -(S51 * d1 + S52 * d2)
    im2 = S51 * d2 - S52 * d1
    return re0, re1, im1, re2, im2


def dft15(x):
    columns = [dft3(*[x[(5 * n1 + 3 * n2) % 15] for n1 in range(3)]) for n2 in range(5)]
    z = dft5([c[0] for c in columns])
    u = dft5([c[1] for c in columns])
    v = dft5([c[2] for c in columns])
    out = {}
    out[(0, 0)] = (z[0], None)
    out[(0, 1)] = (z[1], z[2])
    out[(0, 2)] = (z[3], z[4])
    out[(1, 0)] = (u[0], v[0])
    for j, (b, s) in ((1, (1, 2)), (2, (3, 4))):
        out[(1, j)] = (u[b] - v[s], u[s] + v[b])
        out[(1, 5 - j)] = (u[b] + v[s], v[b] - u[s])
    bins = [None] * 8
    for (k1, k2), (re, im) in out.items():
        k = (10 * k1 + 6 * k2) % 15
        if k <= 7:
            bins[k] = (re, im)
        else:
            bins[15 - k] = (re, -im)
    return bins


def spectra(rows, last, off_ref, x_ref, both_ref, twiddle_ref, band_ref, o_ref, hi_ref, lo_ref, re_ref, im_ref):
    off = off_ref[0]
    lane = lax.broadcasted_iota(jnp.int32, (16, LANES), 1)

    def put(row, c0, a0, value):
        hi, lo = split(value)
        hi_ref[pl.ds(row * LANES + c0, 16), pl.ds(a0, LANES)] = hi
        lo_ref[pl.ds(row * LANES + c0, 16), pl.ds(a0, LANES)] = lo

    extra = rows - PARTS

    def block(i, carry):
        c0 = pl.multiple_of(i * 16, 16)

        def load(j):
            return x_ref[pl.ds(c0 * rows + j, 16, stride=rows), :]

        for t in range(L // LANES):
            x = []
            for b in range(M):
                j = b * (L // LANES) + t
                value = load(j)
                if j < extra:
                    value = jnp.where(lane + j * LANES < off, load(j + PARTS), value)
                x.append(value)
            bins = dft15(x)
            a0 = t * LANES
            put(0, c0, a0, bins[0][0])
            for r in range(1, 8):
                re, im = bins[r]
                cos = twiddle_ref[2 * r - 2, :, a0 : a0 + LANES]
                sin = twiddle_ref[2 * r - 1, :, a0 : a0 + LANES]
                cos = jnp.concatenate([cos, cos], 0)
                sin = jnp.concatenate([sin, sin], 0)
                put(2 * r - 1, c0, a0, re * cos + im * sin)
                put(2 * r, c0, a0, im * cos - re * sin)
        return carry

    lax.fori_loop(0, LANES // 16, block, 0)

    nt = (((1,), (1,)), ((), ()))

    def second(row, count):
        window = slice(row * LANES, (row + count) * LANES)
        p = lax.dot_general(both_ref[...], hi_ref[window, :], nt, preferred_element_type=jnp.float32)
        s = lax.dot_general(both_ref[: 2 * NQ, :], lo_ref[window, :], nt, preferred_element_type=jnp.float32)
        return p[: 2 * NQ] + p[2 * NQ :] + s

    z = second(0, 1)
    re_ref[pl.ds(START, NQ, stride=M), :] = z[:NQ]
    im_ref[pl.ds(START, NQ, stride=M), :] = -z[NQ:]
    for r in range(1, 8):
        z = second(2 * r - 1, 2)
        rc, rs = z[:NQ, :LANES], z[NQ:, :LANES]
        ic, is_ = z[:NQ, LANES:], z[NQ:, LANES:]
        re_ref[pl.ds(START + r, NQ, stride=M), :] = rc + is_
        im_ref[pl.ds(START + r, NQ, stride=M), :] = ic - rs
        re_ref[pl.ds(START - r, NQ, stride=M), :] = rc - is_
        im_ref[pl.ds(START - r, NQ, stride=M), :] = -ic - rs
    re = re_ref[BASE : BASE + FB, :]
    im = im_ref[BASE : BASE + FB, :]
    hi, lo = split(jnp.sqrt(re * re + im * im))
    total = jnp.dot(band_ref[...], jnp.concatenate([hi, lo], 1), preferred_element_type=jnp.float32)
    k = lax.broadcasted_iota(jnp.int32, (FB, LANES), 0)
    count = jnp.minimum(k + SMOOTH, FB - 1) - jnp.maximum(k - SMOOTH, 0) + 1
    smooth = (total[:, :LANES] + total[:, LANES:]) / count.astype(jnp.float32)
    scale = 1.0 / (smooth + 1e-06)
    re, im = re * scale, im * scale
    if not last:
        o_ref[:, :LANES] = re
        o_ref[:, LANES:] = im
    else:
        low = lax.broadcasted_iota(jnp.int32, (FB, LANES), 1) < LANES // 2
        o_ref[...] = jnp.where(low, re, pltpu.roll(im, LANES // 2, 1))


def whiten(records, offsets, t):
    chans = records.shape[0]
    rows = records.shape[2] // LANES
    flat = records.reshape(chans * rows, LANES)
    both, twiddle, band = tables()
    last = (t + 1) * LANES > chans
    lanes = LANES if last else 2 * LANES
    keep = lambda shape: pl.BlockSpec(shape, lambda i: (0,) * len(shape))
    return pl.pallas_call(
        functools.partial(spectra, rows, last),
        grid=(1,),
        in_specs=[
            pl.BlockSpec(memory_space=pltpu.SMEM),
            pl.BlockSpec((LANES * rows, LANES), lambda i: (t, 0)),
            keep(both.shape),
            keep(twiddle.shape),
            keep(band.shape),
        ],
        out_specs=keep((FB, lanes)),
        out_shape=jax.ShapeDtypeStruct((FB, lanes), jnp.float32),
        scratch_shapes=[
            pltpu.VMEM((M * LANES, L), jnp.bfloat16),
            pltpu.VMEM((M * LANES, L), jnp.bfloat16),
            pltpu.VMEM((ROWS + 8, LANES), jnp.float32),
            pltpu.VMEM((ROWS + 8, LANES), jnp.float32),
        ],
        compiler_params=pltpu.CompilerParams(vmem_limit_bytes=56 << 20),
        cost_estimate=pl.CostEstimate(flops=4 * 10**9, bytes_accessed=16 << 20, transcendentals=0),
        name=f"whiten{t}",
    )(offsets, flat, jnp.asarray(both), jnp.asarray(twiddle), jnp.asarray(band))


KB = 8


def pairing(wins, last, scale, *refs):
    a_refs, (b_ref, e_ref), (o_ref, x_ref) = refs[:wins], refs[wins : wins + 2], refs[-2:]
    if not last:
        re = [a[:, :LANES] for a in a_refs]
        im = [a[:, LANES:] for a in a_refs]
    else:
        re = [a[...] for a in a_refs]
        im = [pltpu.roll(a, LANES // 2, 1) for a in re]
    hi, lo = split(jnp.concatenate(re + im, 0))
    lhs = jnp.concatenate([hi, lo], 1)
    x_ref[...] = jnp.dot(lhs, e_ref[...], preferred_element_type=jnp.float32)
    for tile in range(x_ref.shape[1] // LANES):
        lanes = slice(tile * LANES, (tile + 1) * LANES)
        ar = [x_ref[w * KB : (w + 1) * KB, lanes] for w in range(wins)]
        ai = [x_ref[(wins + w) * KB : (wins + w + 1) * KB, lanes] for w in range(wins)]
        for rnd in range(ROUNDS):
            real = imag = None
            for w in range(wins):
                br, bi = b_ref[rnd, w, 0], b_ref[rnd, w, 1]
                p = ar[w] * br + ai[w] * bi
                q = ai[w] * br - ar[w] * bi
                real = p if real is None else real + p
                imag = q if imag is None else imag + q
            o_ref[rnd, :, 0, lanes] = real * scale
            o_ref[rnd, :, 1, lanes] = imag * scale


def correlate(blocks, sources, t, chans, out):
    wins = len(blocks)
    bins, wide = blocks[0].shape
    last = wide == LANES
    width = LANES * SRC // 2 if last else LANES * SRC
    spread = (np.arange(LANES)[:, None] == np.arange(width)[None, :] // SRC).astype(jnp.bfloat16)
    spread = np.concatenate([spread, spread])
    place = t * LANES * SRC // width
    args = [*blocks, sources, jnp.asarray(spread)]
    specs = [pl.BlockSpec((KB, wide), lambda i: (i, 0))] * wins + [
        pl.BlockSpec((ROUNDS, wins, 2, KB, LANES), lambda i: (0, 0, 0, i, 0)),
        pl.BlockSpec(spread.shape, lambda i: (0, 0)),
    ]
    aliases = {}
    if out is not None:
        aliases = {len(args): 0}
        args.append(out)
        specs.append(pl.BlockSpec(memory_space=pl.ANY))
    return pl.pallas_call(
        functools.partial(pairing, wins, last, 1.0 / wins),
        grid=(bins // KB,),
        in_specs=specs,
        out_specs=pl.BlockSpec((ROUNDS, KB, 2, width), lambda i: (0, i, 0, place)),
        out_shape=jax.ShapeDtypeStruct((ROUNDS, bins, 2, chans * SRC), jnp.float32),
        scratch_shapes=[pltpu.VMEM((2 * wins * KB, width), jnp.float32)],
        input_output_aliases=aliases,
        compiler_params=pltpu.CompilerParams(vmem_limit_bytes=40 << 20),
        cost_estimate=pl.CostEstimate(flops=10**9, bytes_accessed=12 << 20, transcendentals=0),
        name=f"pairing{t}",
    )(*args)


def passed_along(block, axis, distance):
    devices = range(lax.axis_size(axis))
    route = [((i - distance) % len(devices), i) for i in devices]
    return lax.ppermute(block, axis, route)


def shards(records, offsets):
    chans = records.shape[0]
    assert records.shape[1] == 1
    n = lax.axis_size("tm")
    me = lax.axis_index("tm")
    bins = FB // n
    chunks = []
    for t in range(-(-chans // LANES)):
        white = whiten(records, offsets, t)
        blocks = []
        for shift in range(n):
            rows = lax.rem(me + shift, n) * bins
            block = lax.dynamic_slice_in_dim(white, rows, bins, 0)
            blocks.append(passed_along(block, "tm", shift) if shift else block)
        chunks.append(blocks)
    own = jnp.stack([b[:, c : c + SRC] for b in chunks[0] for c in (0, LANES)])
    flat = own.reshape(-1, LANES)
    got = [passed_along(flat, "chan", -rnd) for rnd in range(1, ROUNDS + 1)]
    sources = jnp.stack(got).reshape(ROUNDS, n, 2, bins, SRC)
    sources = jnp.tile(sources, (1, 1, 1, 1, LANES // SRC))
    out = None
    for t, blocks in enumerate(chunks):
        out = correlate(blocks, sources, t, chans, out)
    return out


def solution(mesh):
    return jax.shard_map(
        shards,
        mesh=mesh,
        in_specs=(P("chan", "tm", None), P("tm")),
        out_specs=P(None, "tm", None, "chan"),
        check_vma=False,
    )
```
